32 devices in a mesh: col: 4 (over y, x), dev: 4 (over z), ao: 2 (over core).
Axes of the slice: x: 2, y: 2, z: 4, core: 2. Of those that a mesh axis runs over, the one named last changes fastest.
Arguments:
- raw_ints: bfloat16 [1024, 32, 512], P('dev', None, 'col'), may hold values from -1.078125 to 1.078125
- metric: bfloat16 [1024, 1024], P('dev'), may hold values from -0.1875 to 0.1875
- amplitudes: bfloat16 [512, 512, 2048], P('col', 'dev', 'ao'), may hold values from -0.017944336 to 0.017944336
- pair_list: int32 [2, 2048], P(None, 'ao'), may hold values from 0 to 63
- occ_energy: float32 [64], replicated, may hold values from -2 to -0.3
- vir_energy: float32 [512], replicated, may hold values from 0.2 to 3
- window_ids: int32 [32], replicated, may hold values from 0 to 511, as said below
Outputs:
- residual: float32 [1024, 2048], P(('col', 'dev'), 'ao')
The draws below stay inside these ranges and needn't reach their ends.
Inputs may be any that keep to these rules, and one draw needn't show every extreme that they name: `window_ids`: distinct virtual orbitals; 0 and 511 are always among them.
All inputs are finite; a program needn't handle non-finite values.
Results may differ from the reference program's by a relative error of at most 0.0041.
Values may be sent and summed in bfloat16 or wider, within the bound.
No kernel may reach another device: no remote copies, remote signals or barrier semaphores. Data moves between devices by JAX's collectives and lax.ppermute only.
A program may use at most 192 MiB of HBM per device.

```python
import jax
import jax.numpy as jnp
from jax import lax

NV = 512
NAUX = 1024
NOCC = 64
W = 32
NPAIRS = 2048


def draw_window_ids(key, part):
    middle_ids = jax.random.permutation(key, NV - 2)[:W - 2] + 1
    combined = jnp.concatenate([jnp.array([0, NV - 1], dtype=jnp.int32), middle_ids.astype(jnp.int32)])
    return jax.random.permutation(jax.random.fold_in(key, 7), combined).astype(jnp.int32)


def set_ends(result, stream_key, least, high):
    dims = result.shape
    place = [jax.random.randint(jax.random.fold_in(stream_key, axis), (), 0, dims[axis]) for axis in range(len(dims))]
    result = result.at[tuple(place)].set(least)
    longest = dims.index(max(dims))
    place[longest] = (place[longest] + 1) % dims[longest]
    return result.at[tuple(place)].set(high)


def shard_levels(stream_key, extent, split, smallest, high):
    gain, own = 1.0, jax.random.fold_in(stream_key, 6)
    for axis_at, shards_of in split:
        steps = jnp.exp(jax.random.uniform(jax.random.fold_in(own, axis_at), (shards_of,), jnp.float32, smallest / len(split), high / len(split)))
        gain = gain * jnp.repeat(steps, extent[axis_at] // shards_of).reshape([-1 if axis == axis_at else 1 for axis in range(len(extent))])
    return gain


def bell_draw(key, extent, scale, reach, cuts=(), kind=jnp.bfloat16):
    gain = shard_levels(key, extent, cuts, -0.22, 0.18) if cuts else 1.0
    values = jax.random.normal(key, extent, jnp.float32) * scale * gain
    return jnp.minimum(jnp.maximum(values, -reach), reach).astype(kind)


def setup_inputs(seed: int = 0) -> dict:
    keys = jax.random.split(jax.random.key(seed), 8)
    raw_ints = bell_draw(keys[0], (NAUX, W, NV), 0.18, 1.078125, ((0, 4), (2, 4)))
    metric = bell_draw(keys[1], (NAUX, NAUX), NAUX ** -0.5, 0.1875, ((0, 4),))
    amplitudes = bell_draw(keys[2], (NV, NV, NPAIRS), 0.003, 0.017944336, ((0, 4), (1, 4), (2, 2)))
    pair_list = set_ends(jax.random.randint(keys[3], (2, NPAIRS), 0, NOCC), jax.random.fold_in(keys[3], 1), 0, NOCC - 1).astype(jnp.int32)
    occ_energy = jnp.clip(jax.random.uniform(keys[4], (NOCC,), jnp.float32, -2.0, -0.3), -2.0, -0.3)
    vir_energy = jnp.clip(jax.random.uniform(keys[5], (NV,), jnp.float32, 0.2, 3.0), 0.2, 3.0)
    window_ids = draw_window_ids(jax.random.fold_in(keys[7], 71), 0)
    return dict(raw_ints=raw_ints, metric=metric, amplitudes=amplitudes, pair_list=pair_list, occ_energy=occ_energy, vir_energy=vir_energy, window_ids=window_ids)


def reference(raw_ints, metric, amplitudes, pair_list, occ_energy, vir_energy, window_ids):
    flat_factors = jnp.dot(metric, raw_ints.reshape(NAUX, W * NV), preferred_element_type=jnp.float32).astype(jnp.bfloat16)
    cube = flat_factors.reshape(NAUX, W, NV)
    amp_matrix = amplitudes.reshape(NV * NV, NPAIRS)

    def ladder_row(column):
        right_side = lax.dynamic_index_in_dim(cube, column, 1, keepdims=False)
        integrals = lax.dot_general(flat_factors, right_side, (((0,), (0,)), ((), ())), preferred_element_type=jnp.float32)
        integrals = integrals.astype(jnp.bfloat16).reshape(W, NV * NV)
        return jnp.dot(integrals, amp_matrix, preferred_element_type=jnp.float32)

    stacked = lax.map(ladder_row, jnp.arange(W, dtype=jnp.int32))
    summed = jnp.transpose(stacked, (1, 0, 2)).reshape(W * W, NPAIRS)
    energy_i = occ_energy[pair_list[0]]
    energy_j = occ_energy[pair_list[1]]
    window_energy = vir_energy[window_ids]
    energy_first = jnp.repeat(window_energy, W)
    energy_second = jnp.tile(window_energy, W)
    denominator = (energy_i + energy_j)[None, :] - (energy_first + energy_second)[:, None]
    return summed / denominator
```

```python
import jax
import jax.numpy as jnp
from jax import lax
from jax.experimental import pallas as pl
from jax.experimental.pallas import tpu as pltpu
from jax.sharding import PartitionSpec as P


def select_energy(positions, table):
    labels = jnp.arange(table.shape[0], dtype=jnp.int32)
    return jnp.sum(jnp.where(positions[:, None] == labels[None, :], table[None, :], 0.0), axis=1)


def general_plan(raw_ints, metric, amplitudes, pair_list, occ_energy, vir_energy, window_ids):
    full_width = raw_ints.shape[1]
    portion = full_width // lax.axis_size("ao")
    own_rows = lax.dynamic_slice_in_dim(raw_ints, lax.axis_index("ao") * portion, portion, 1)
    local_aux = metric.shape[0]
    rows_used = own_rows.shape[1]
    c_block = own_rows.shape[2]
    raw_block = lax.all_gather(own_rows, "dev", axis=0, tiled=True)
    row_count = raw_block.shape[0]
    transformed = jnp.dot(
        metric,
        raw_block.reshape(row_count, rows_used * c_block),
        preferred_element_type=jnp.float32,
    )
    transformed = transformed.astype(jnp.bfloat16).reshape(local_aux, rows_used, c_block)
    spread = lax.all_gather(transformed, "col", axis=2, tiled=True)
    right_factor = lax.all_to_all(spread, "dev", split_axis=2, concat_axis=0, tiled=True)
    d_block = right_factor.shape[2]
    contract = (((0,), (0,)), ((), ()))
    left_factor = lax.all_gather(transformed, "dev", axis=0, tiled=True)
    right_factor = lax.all_gather(right_factor, "ao", axis=1, tiled=True)
    all_aux = left_factor.shape[0]
    own_ladder = lax.dot_general(
        left_factor.reshape(all_aux, rows_used * c_block),
        right_factor.reshape(all_aux, full_width * d_block),
        contract,
        preferred_element_type=jnp.float32,
    )
    ladder_flat = lax.all_gather(own_ladder.astype(jnp.bfloat16), "ao", axis=0, tiled=True)
    ladder = ladder_flat.reshape(full_width, c_block, full_width, d_block)
    ladder = jnp.transpose(ladder, (0, 2, 1, 3)).reshape(full_width * full_width, c_block * d_block)
    partial_value = jnp.dot(
        ladder,
        amplitudes.reshape(c_block * d_block, amplitudes.shape[2]),
        preferred_element_type=jnp.float32,
    )
    summed = lax.psum_scatter(partial_value, ("col", "dev"), scatter_dimension=0, tiled=True)
    row_total = summed.shape[0]
    global_rows = lax.axis_index(("col", "dev")) * row_total + jnp.arange(
        row_total, dtype=jnp.int32
    )
    window_energy = select_energy(window_ids, vir_energy)
    energy_first = select_energy(global_rows // full_width, window_energy)
    energy_second = select_energy(global_rows % full_width, window_energy)
    energy_i = select_energy(pair_list[0], occ_energy)
    energy_j = select_energy(pair_list[1], occ_energy)
    denominator = (energy_i + energy_j)[None, :] - (energy_first + energy_second)[:, None]
    return summed / denominator


def cycle_order(count):
    if count & (count - 1):
        return list(range(count))
    return [place ^ (place >> 1) for place in range(count)]


def pass_round(piece, axis):
    count = lax.axis_size(axis)
    pairs = [(place, (place + 1) % count) for place in range(count)]
    pieces = [piece]
    for _ in range(count - 1):
        pieces.append(lax.ppermute(pieces[-1], axis, pairs))
    return pieces


def swap_cores(piece):
    return lax.ppermute(piece, "ao", [(0, 1), (1, 0)])


def from_diagonal(piece, turn):
    cols, devs = lax.axis_size("col"), lax.axis_size("dev")
    order = cycle_order(cols)
    held = piece
    source = lax.axis_index("col") == lax.axis_index("dev")
    total = jnp.where(source, piece, jnp.zeros_like(piece))
    for hop in range(cols - 1):
        pairs = []
        for dev in range(devs):
            first = order.index(dev)
            sender = order[(first + turn * hop) % cols]
            taker = order[(first + turn * (hop + 1)) % cols]
            pairs.append((sender * devs + dev, taker * devs + dev))
        held = lax.ppermute(held, ("col", "dev"), pairs)
        total = total + held
    return total


def whole_metric(metric):
    cols, cores = lax.axis_size("col"), lax.axis_size("ao")
    devs = lax.axis_size("dev")
    share = metric.shape[0] // (cols * cores)
    at = (lax.axis_index("col") * cores + lax.axis_index("ao")) * share
    own = lax.dynamic_slice_in_dim(metric, at, share, 0)
    rows = jnp.concatenate(pass_round(own, "dev"), axis=0)
    order = cycle_order(cols)
    pairs = [(order[place], order[(place + 1) % cols]) for place in range(cols)]
    pieces = [rows]
    for _ in range(cols - 1):
        pieces.append(lax.ppermute(pieces[-1], "col", pairs))
    rows = jnp.concatenate(pieces, axis=0)
    other = swap_cores(rows)
    first = lax.axis_index("ao") == 0
    rows = jnp.concatenate([jnp.where(first, rows, other), jnp.where(first, other, rows)], axis=0)
    block = metric.shape[1] // devs
    blocks = [
        lax.dynamic_slice_in_dim(rows, (lax.axis_index("dev") - step) % devs * block, block, 1)
        for step in range(devs)
    ]
    return jnp.concatenate(blocks, axis=1)


def ladder_kernel(own_ref, other_ref, right_ref, ladder_ref):
    c_count, width, depth = own_ref.shape
    d_block = ladder_ref.shape[1] // c_count
    right_rows = right_ref.shape[1] // d_block
    for half, ref in enumerate((own_ref, other_ref)):
        product = jnp.dot(
            ref[...].reshape(c_count * width, depth),
            right_ref[...],
            preferred_element_type=jnp.float32,
        ).astype(jnp.bfloat16)
        for c in range(c_count):
            for b in range(right_rows):
                row = (b * 2 + half) * width
                ladder_ref[row : row + width, c * d_block : (c + 1) * d_block] = product[
                    c * width : (c + 1) * width, b * d_block : (b + 1) * d_block
                ]


def ladder_of(own_left, other_left, right, d_block):
    c_block, width, depth = own_left.shape
    right_rows = right.shape[1] // d_block
    step = 16
    left_spec = pl.BlockSpec((step, width, depth), lambda i: (i, 0, 0))
    rows = right_rows * 2 * width
    return pl.pallas_call(
        ladder_kernel,
        grid=(c_block // step,),
        in_specs=[left_spec, left_spec, pl.BlockSpec(right.shape, lambda i: (0, 0))],
        out_specs=pl.BlockSpec((rows, step * d_block), lambda i: (0, i)),
        out_shape=jax.ShapeDtypeStruct((rows, c_block * d_block), jnp.bfloat16),
        compiler_params=pltpu.CompilerParams(vmem_limit_bytes=50 * 1024 * 1024),
        cost_estimate=pl.CostEstimate(
            flops=4 * c_block * width * depth * right.shape[1],
            bytes_accessed=2 * (2 * own_left.size + right.size + rows * c_block * d_block),
            transcendentals=0,
        ),
    )(own_left, other_left, right)


def share_out(partial):
    cols, devs = lax.axis_size("col"), lax.axis_size("dev")
    rows, _, pairs = partial.shape
    me = lax.axis_index("col")
    split = partial.reshape(rows, cols, devs, pairs)

    def slab(place):
        return lax.dynamic_index_in_dim(split, place, 1, keepdims=False)

    parts = [slab(me)]
    for turn in range(1, cols):
        links = [(col, col ^ turn) for col in range(cols)]
        parts.append(lax.ppermute(slab(me ^ turn), "col", links))
    plane = sum(part.astype(jnp.float32) for part in parts)
    here = lax.axis_index("dev")
    total = lax.dynamic_index_in_dim(plane, here, 1, keepdims=False)
    narrow = plane.astype(jnp.bfloat16)
    for turn in range(1, devs):
        links = [(dev, dev ^ turn) for dev in range(devs)]
        sent = lax.dynamic_index_in_dim(narrow, here ^ turn, 1, keepdims=False)
        total = total + lax.ppermute(sent, "dev", links).astype(jnp.float32)
    return total


def plan_on_device(raw_ints, metric, amplitudes, pair_list, occ_energy, vir_energy, window_ids):
    aux, full_width, c_block = raw_ints.shape
    cols, devs = lax.axis_size("col"), lax.axis_size("dev")
    core = lax.axis_index("ao")
    width = full_width // 2
    own = lax.dynamic_index_in_dim(raw_ints.reshape(aux, width, 2, c_block), core, 2, keepdims=False)
    half = aux // 2
    chains = [pass_round(own[:half], "dev"), pass_round(own[half:], "dev")]
    metric_all = whole_metric(metric)
    raw_left = jnp.concatenate([chains[h][s] for s in range(devs) for h in range(2)], axis=0)
    raw_right = jnp.concatenate(
        [from_diagonal(chains[h][s], 1 - 2 * h) for s in range(devs) for h in range(2)], axis=0
    )
    all_aux = raw_left.shape[0]
    own_left = lax.dot_general(
        raw_left, metric_all, (((0,), (1,)), ((), ())), preferred_element_type=jnp.float32
    ).astype(jnp.bfloat16)
    own_left = jnp.transpose(own_left, (1, 0, 2))
    other_left = swap_cores(own_left)
    right = jnp.dot(
        metric_all, raw_right.reshape(all_aux, width * c_block), preferred_element_type=jnp.float32
    ).astype(jnp.bfloat16)
    own_ladder = ladder_of(own_left, other_left, right, c_block)
    other_ladder = swap_cores(own_ladder)
    flat_amplitudes = amplitudes.reshape(c_block * amplitudes.shape[1], amplitudes.shape[2])
    sums = []
    for ladder in (own_ladder, other_ladder):
        partial = jnp.dot(ladder, flat_amplitudes, preferred_element_type=jnp.float32)
        partial = partial.astype(jnp.bfloat16).reshape(2 * width, width, partial.shape[1])
        sums.append(share_out(partial).reshape(width, 2, partial.shape[2]))
    (own_same, own_cross), (other_same, other_cross) = [(s[:, 0], s[:, 1]) for s in sums]
    first = core == 0

    def by_core(zero, one):
        return jnp.where(first, zero, one)

    even_a = jnp.stack([by_core(own_same, other_same), by_core(other_cross, own_cross)], axis=1)
    odd_a = jnp.stack([by_core(own_cross, other_cross), by_core(other_same, own_same)], axis=1)
    summed = jnp.stack([even_a, odd_a]).reshape(2 * full_width, amplitudes.shape[2])
    row_total = summed.shape[0]
    global_rows = lax.axis_index(("col", "dev")) * row_total + jnp.arange(
        row_total, dtype=jnp.int32
    )
    window_energy = select_energy(window_ids, vir_energy)
    energy_first = select_energy(global_rows // full_width, window_energy)
    energy_second = select_energy(global_rows % full_width, window_energy)
    energy_i = select_energy(pair_list[0], occ_energy)
    energy_j = select_energy(pair_list[1], occ_energy)
    denominator = (energy_i + energy_j)[None, :] - (energy_first + energy_second)[:, None]
    return summed / denominator


def on_device(raw_ints, *rest):
    cols, devs, cores = lax.axis_size("col"), lax.axis_size("dev"), lax.axis_size("ao")
    aux, full_width, c_block = raw_ints.shape
    paired = cols == devs and cores == 2 and full_width == 2 * cols * devs
    if paired and cols & (cols - 1) == 0 and c_block % 128 == 0:
        return plan_on_device(raw_ints, *rest)
    return general_plan(raw_ints, *rest)


def solution(mesh):
    in_specs = (
        P("dev", None, "col"),
        P("dev", None),
        P("col", "dev", "ao"),
        P(None, "ao"),
        P(),
        P(),
        P(),
    )
    out_specs = P(("col", "dev"), "ao")
    return jax.shard_map(
        on_device, mesh=mesh, in_specs=in_specs, out_specs=out_specs, check_vma=False
    )
```

```python
import functools

import jax
import jax.numpy as jnp
from jax import lax
from jax.experimental import pallas as pl
from jax.experimental.pallas import tpu as pltpu
from jax.sharding import PartitionSpec as P


def select_energy(positions, table):
    labels = jnp.arange(table.shape[0], dtype=jnp.int32)
    return jnp.sum(jnp.where(positions[:, None] == labels[None, :], table[None, :], 0.0), axis=1)


def general_plan(raw_ints, metric, amplitudes, pair_list, occ_energy, vir_energy, window_ids):
    full_width = raw_ints.shape[1]
    portion = full_width // lax.axis_size("ao")
    own_rows = lax.dynamic_slice_in_dim(raw_ints, lax.axis_index("ao") * portion, portion, 1)
    local_aux = metric.shape[0]
    rows_used = own_rows.shape[1]
    c_block = own_rows.shape[2]
    raw_block = lax.all_gather(own_rows, "dev", axis=0, tiled=True)
    row_count = raw_block.shape[0]
    transformed = jnp.dot(
        metric,
        raw_block.reshape(row_count, rows_used * c_block),
        preferred_element_type=jnp.float32,
    )
    transformed = transformed.astype(jnp.bfloat16).reshape(local_aux, rows_used, c_block)
    spread = lax.all_gather(transformed, "col", axis=2, tiled=True)
    right_factor = lax.all_to_all(spread, "dev", split_axis=2, concat_axis=0, tiled=True)
    d_block = right_factor.shape[2]
    contract = (((0,), (0,)), ((), ()))
    left_factor = lax.all_gather(transformed, "dev", axis=0, tiled=True)
    right_factor = lax.all_gather(right_factor, "ao", axis=1, tiled=True)
    all_aux = left_factor.shape[0]
    own_ladder = lax.dot_general(
        left_factor.reshape(all_aux, rows_used * c_block),
        right_factor.reshape(all_aux, full_width * d_block),
        contract,
        preferred_element_type=jnp.float32,
    )
    ladder_flat = lax.all_gather(own_ladder.astype(jnp.bfloat16), "ao", axis=0, tiled=True)
    ladder = ladder_flat.reshape(full_width, c_block, full_width, d_block)
    ladder = jnp.transpose(ladder, (0, 2, 1, 3)).reshape(full_width * full_width, c_block * d_block)
    partial_value = jnp.dot(
        ladder,
        amplitudes.reshape(c_block * d_block, amplitudes.shape[2]),
        preferred_element_type=jnp.float32,
    )
    summed = lax.psum_scatter(partial_value, ("col", "dev"), scatter_dimension=0, tiled=True)
    row_total = summed.shape[0]
    global_rows = lax.axis_index(("col", "dev")) * row_total + jnp.arange(
        row_total, dtype=jnp.int32
    )
    window_energy = select_energy(window_ids, vir_energy)
    energy_first = select_energy(global_rows // full_width, window_energy)
    energy_second = select_energy(global_rows % full_width, window_energy)
    energy_i = select_energy(pair_list[0], occ_energy)
    energy_j = select_energy(pair_list[1], occ_energy)
    denominator = (energy_i + energy_j)[None, :] - (energy_first + energy_second)[:, None]
    return summed / denominator


VMEM = 62 * 1024 * 1024


def on_ring(piece, axis):
    count = lax.axis_size(axis)
    pairs = [(place, (place + 1) % count) for place in range(count)]
    return lax.ppermute(piece, axis, pairs)


def flip(piece, axis, bit):
    pairs = [(place, place ^ 1 << bit) for place in range(lax.axis_size(axis))]
    return lax.ppermute(piece, axis, pairs)


def bits_of(count):
    return count.bit_length() - 1


def metric_kernel(devs, place_ref, *refs):
    whole_ref, turned_ref = refs[-2:]
    pieces = refs[:-2]
    count = len(pieces) // 2
    rows, aux = pieces[0].shape
    core, dev = place_ref[0], place_ref[1]
    block = aux // devs
    for half in range(2):
        for at in range(count):
            row = pl.multiple_of(((core ^ half) * count + at) * rows, rows)
            for step in range(devs):
                column = pl.multiple_of(lax.rem(dev - step + devs, devs) * block, block)
                whole_ref[pl.ds(row, rows), step * block : (step + 1) * block] = pieces[
                    half * count + at
                ][:, pl.ds(column, block)]
    turned_ref[...] = whole_ref[...].T


def whole_metric(metric):
    cols, devs, cores = lax.axis_size("col"), lax.axis_size("dev"), lax.axis_size("ao")
    share = metric.shape[0] // (cols * cores)
    at = (lax.axis_index("col") * cores + lax.axis_index("ao")) * share
    shares = [lax.dynamic_slice_in_dim(metric, at, share, 0)]
    for step in range(1, devs):
        pairs = [(dev, (dev + step) % devs) for dev in range(devs)]
        shares.append(lax.ppermute(shares[0], "dev", pairs))
    rows = [jnp.concatenate(shares, axis=0)]
    for turn in range(1, cols):
        rows.append(lax.ppermute(rows[0], "col", [(col, col ^ turn) for col in range(cols)]))
    rows += [flip(rows[turn], "ao", 0) for turn in range(cols)]
    place = jnp.stack([lax.axis_index("ao"), lax.axis_index("dev")]).astype(jnp.int32)
    shape = jax.ShapeDtypeStruct((metric.shape[0] * devs, metric.shape[1]), metric.dtype)
    return pl.pallas_call(
        functools.partial(metric_kernel, devs),
        in_specs=[pl.BlockSpec(memory_space=pltpu.SMEM)]
        + [pl.BlockSpec(memory_space=pltpu.VMEM)] * len(rows),
        out_specs=[pl.BlockSpec(memory_space=pltpu.VMEM)] * 2,
        out_shape=[shape, jax.ShapeDtypeStruct(shape.shape[::-1], metric.dtype)],
        compiler_params=pltpu.CompilerParams(vmem_limit_bytes=VMEM),
    )(place, *rows)


def left_kernel(metric_ref, *refs):
    rows = jnp.concatenate([ref[...] for ref in refs[:-1]], axis=2)
    count, width, depth = rows.shape
    product = jnp.dot(
        rows.reshape(count * width, depth), metric_ref[...], preferred_element_type=jnp.float32
    )
    refs[-1][...] = product.astype(jnp.bfloat16).reshape(count, width, product.shape[1])


def fit_left(metric_turned, pieces):
    c_block, width, depth = pieces[0].shape
    step = 32
    aux = metric_turned.shape[1]
    piece_spec = pl.BlockSpec((step, width, depth), lambda i: (i, 0, 0))
    return pl.pallas_call(
        left_kernel,
        grid=(c_block // step,),
        in_specs=[pl.BlockSpec(metric_turned.shape, lambda i: (0, 0))] + [piece_spec] * len(pieces),
        out_specs=pl.BlockSpec((step, width, aux), lambda i: (i, 0, 0)),
        out_shape=jax.ShapeDtypeStruct((c_block, width, aux), jnp.bfloat16),
        compiler_params=pltpu.CompilerParams(vmem_limit_bytes=VMEM),
        cost_estimate=pl.CostEstimate(
            flops=2 * metric_turned.size * c_block * width,
            bytes_accessed=2 * (metric_turned.size + 2 * c_block * width * aux),
            transcendentals=0,
        ),
    )(metric_turned, *pieces)


def fit_kernel(arrived_ref, metric_ref, *refs):
    out_ref, held, sems = refs[-3:]
    pieces = refs[:-3]
    count = len(pieces) // 2
    width = held.shape[2]
    step = pl.program_id(0)

    def fetch(at, slot):
        for piece in range(count):
            for came in range(2):

                @pl.when(arrived_ref[piece % 2] == came)
                def _(piece=piece, came=came):
                    pltpu.make_async_copy(
                        pieces[2 * piece + came].at[pl.ds(at * width, width)],
                        held.at[slot, piece],
                        sems.at[slot, piece],
                    ).start()

    @pl.when(step == 0)
    def _():
        fetch(0, 0)

    slot = lax.rem(step, 2)

    @pl.when(step + 1 < pl.num_programs(0))
    def _():
        fetch(step + 1, 1 - slot)

    for piece in range(count):
        pltpu.make_async_copy(
            pieces[2 * piece].at[pl.ds(step * width, width)],
            held.at[slot, piece],
            sems.at[slot, piece],
        ).wait()
    columns = [
        jnp.concatenate([held[slot, piece, b] for piece in range(count)], axis=0)
        for b in range(width)
    ]
    out_ref[...] = jnp.dot(
        metric_ref[...], jnp.concatenate(columns, axis=1), preferred_element_type=jnp.float32
    ).astype(out_ref.dtype)


def fit_right(arrived, metric_all, flat):
    width, depth, d_block = flat[0].shape
    step = 4
    aux = metric_all.shape[0]
    count = len(flat) // 2
    part = count * depth
    return pl.pallas_call(
        fit_kernel,
        grid=(width // step,),
        in_specs=[
            pl.BlockSpec(memory_space=pltpu.SMEM),
            pl.BlockSpec((aux, part), lambda i: (0, 0)),
        ]
        + [pl.BlockSpec(memory_space=pl.ANY)] * len(flat),
        out_specs=pl.BlockSpec((aux, step * d_block), lambda i: (0, i)),
        out_shape=jax.ShapeDtypeStruct((aux, width * d_block), jnp.float32),
        scratch_shapes=[
            pltpu.VMEM((2, count, step, depth, d_block), jnp.bfloat16),
            pltpu.SemaphoreType.DMA((2, count)),
        ],
        compiler_params=pltpu.CompilerParams(vmem_limit_bytes=24 * 1024 * 1024),
        cost_estimate=pl.CostEstimate(
            flops=2 * aux * part * width * d_block,
            bytes_accessed=2 * (aux * part + count * flat[0].size + 2 * aux * width * d_block),
            transcendentals=0,
        ),
    )(arrived, metric_all, *flat)


def ladder_kernel(
    arrived_ref, metric_ref, own_ref, other_ref, early_ref, *refs
):
    ladder_ref, right_ref, sums_ref, held, sum_sems, sems = refs[-6:]
    pieces = refs[:-6]
    count = len(pieces) // 2
    c_count, width, depth = own_ref.shape
    d_block = ladder_ref.shape[1] // c_count
    right_rows = right_ref.shape[1] // d_block
    parts, _, columns = sums_ref.shape

    @pl.when(pl.program_id(0) == 0)
    def _():
        for piece in range(count):
            for came in range(2):

                @pl.when(arrived_ref[piece % 2] == came)
                def _(piece=piece, came=came):
                    pltpu.make_async_copy(
                        pieces[2 * piece + came], held.at[piece], sems.at[piece]
                    ).start()

        fetched = [
            pltpu.make_async_copy(
                early_ref.at[:, pl.ds(part * columns, columns)], sums_ref.at[part], sum_sems.at[part]
            )
            for part in range(parts)
        ]
        for copy in fetched:
            copy.start()
        for piece in range(count):
            pltpu.make_async_copy(pieces[2 * piece], held.at[piece], sems.at[piece]).wait()
        many = columns // d_block
        for part in range(parts):
            fetched[part].wait()
            late = [
                jnp.concatenate([held[piece, part * many + b] for piece in range(count)], axis=0)
                for b in range(many)
            ]
            product = jnp.dot(
                metric_ref[...], jnp.concatenate(late, axis=1), preferred_element_type=jnp.float32
            )
            right_ref[:, part * columns : (part + 1) * columns] = (
                product + sums_ref[part]
            ).astype(right_ref.dtype)

    for half, ref in enumerate((own_ref, other_ref)):
        product = jnp.dot(
            ref[...].reshape(c_count * width, depth),
            right_ref[...],
            preferred_element_type=jnp.float32,
        ).astype(jnp.bfloat16)
        for c in range(c_count):
            for b in range(right_rows):
                row = (b * 2 + half) * width
                ladder_ref[row : row + width, c * d_block : (c + 1) * d_block] = product[
                    c * width : (c + 1) * width, b * d_block : (b + 1) * d_block
                ]


def ladder_of(arrived, metric_all, own_left, other_left, early, flat):
    c_block, width, depth = own_left.shape
    right_rows, rows_late, d_block = flat[0].shape
    step, parts = 16, 4
    count = len(flat) // 2
    part = count * rows_late
    aux, columns = early.shape
    left_spec = pl.BlockSpec((step, width, depth), lambda i: (i, 0, 0))
    rows = right_rows * 2 * width
    return pl.pallas_call(
        ladder_kernel,
        grid=(c_block // step,),
        in_specs=[
            pl.BlockSpec(memory_space=pltpu.SMEM),
            pl.BlockSpec((aux, part), lambda i: (0, metric_all.shape[1] // part - 1)),
            left_spec,
            left_spec,
        ]
        + [pl.BlockSpec(memory_space=pl.ANY)] * (1 + len(flat)),
        out_specs=pl.BlockSpec((rows, step * d_block), lambda i: (0, i)),
        out_shape=jax.ShapeDtypeStruct((rows, c_block * d_block), jnp.bfloat16),
        scratch_shapes=[
            pltpu.VMEM((aux, columns), jnp.bfloat16),
            pltpu.VMEM((parts, aux, columns // parts), jnp.float32),
            pltpu.VMEM((count, right_rows, rows_late, d_block), jnp.bfloat16),
            pltpu.SemaphoreType.DMA((parts,)),
            pltpu.SemaphoreType.DMA((count,)),
        ],
        compiler_params=pltpu.CompilerParams(vmem_limit_bytes=30 * 1024 * 1024),
        cost_estimate=pl.CostEstimate(
            flops=4 * c_block * width * depth * columns + 2 * aux * part * columns,
            bytes_accessed=2 * (2 * own_left.size + 2 * early.size + rows * c_block * d_block),
            transcendentals=0,
        ),
    )(arrived, metric_all, own_left, other_left, early, *flat)


def contract_kernel(ladder_ref, amplitudes_ref, out_ref, total_ref):
    @pl.when(pl.program_id(0) == 0)
    def _():
        total_ref[...] = jnp.zeros_like(total_ref)

    product = jnp.dot(ladder_ref[...], amplitudes_ref[...], preferred_element_type=jnp.float32)
    tiles, _, lanes = total_ref.shape
    for tile in range(tiles):
        total_ref[tile] += product[:, tile * lanes : (tile + 1) * lanes]

    @pl.when(pl.program_id(0) == pl.num_programs(0) - 1)
    def _():
        owners, rows, _ = out_ref.shape
        for owner in range(owners):
            for tile in range(tiles):
                out_ref[owner, :, tile * lanes : (tile + 1) * lanes] = total_ref[
                    tile, pl.ds(owner, rows, stride=owners), :
                ].astype(out_ref.dtype)


def contract(ladder, amplitudes, owners):
    rows, depth = ladder.shape
    columns = amplitudes.shape[1]
    step = 4096
    return pl.pallas_call(
        contract_kernel,
        grid=(depth // step,),
        in_specs=[
            pl.BlockSpec((rows, step), lambda i: (0, i)),
            pl.BlockSpec((step, columns), lambda i: (i, 0)),
        ],
        out_specs=pl.BlockSpec((owners, rows // owners, columns), lambda i: (0, 0, 0)),
        out_shape=jax.ShapeDtypeStruct((owners, rows // owners, columns), jnp.bfloat16),
        scratch_shapes=[pltpu.VMEM((columns // 128, rows, 128), jnp.float32)],
        compiler_params=pltpu.CompilerParams(vmem_limit_bytes=VMEM),
        cost_estimate=pl.CostEstimate(
            flops=2 * rows * depth * columns,
            bytes_accessed=2 * (rows * depth + depth * columns + rows * columns),
            transcendentals=0,
        ),
    )(ladder, amplitudes)


def spread(partial):
    return lax.all_to_all(partial, ("col", "dev"), split_axis=0, concat_axis=0, tiled=True)


def total_of(parts):
    return jnp.sum(parts.astype(jnp.float32), axis=0)


def plan_on_device(raw_ints, metric, amplitudes, pair_list, occ_energy, vir_energy, window_ids):
    aux, full_width, c_block = raw_ints.shape
    cols, devs = lax.axis_size("col"), lax.axis_size("dev")
    core = lax.axis_index("ao")
    width = full_width // 2
    own = lax.dynamic_index_in_dim(raw_ints.reshape(aux, width, 2, c_block), core, 2, keepdims=False)
    own = jnp.transpose(own, (1, 0, 2))
    half = aux // 2
    here = list(lax.optimization_barrier((own[:, :half], own[:, half:])))
    metric_all, metric_turned = whole_metric(metric)
    away = lax.axis_index("col") ^ lax.axis_index("dev")
    bits = bits_of(cols)
    bit_set = [(away >> bit) & 1 for bit in range(bits)]
    came = [flag == 1 for flag in bit_set]
    *came, away = lax.optimization_barrier((*came, away))
    arrived = jnp.stack([bit_set[(h + bits - 1) % bits] for h in range(2)]).astype(jnp.int32)
    pieces, left_pieces = [], []
    for s in range(devs):
        for h in range(2):
            left_pieces.append(jnp.transpose(here[h], (2, 0, 1)))
        if s < devs - 1:
            ahead = [on_ring(here[h], "dev") for h in range(2)]
        else:
            own_left = fit_left(metric_turned, left_pieces)
        held = here
        for hop in range(bits):
            if hop:
                held = [
                    jnp.where(came[(h + hop - 1) % bits], last[h], held[h]) for h in range(2)
                ]
                held = list(lax.optimization_barrier(tuple(held)))
            last = [flip(held[h], "col", (h + hop) % bits) for h in range(2)]
        pieces += [held[0], last[0], held[1], last[1]]
        here = ahead
    other_left = flip(own_left, "ao", 0)
    early = fit_right(arrived, metric_all, pieces[:-4])
    own_ladder = ladder_of(arrived, metric_all, own_left, other_left, early, pieces[-4:])
    other_ladder = flip(own_ladder, "ao", 0)
    flat_amplitudes = amplitudes.reshape(c_block * amplitudes.shape[1], amplitudes.shape[2])
    own_partial = contract(own_ladder, flat_amplitudes, width)
    own_parts = spread(own_partial)
    other_partial = contract(other_ladder, flat_amplitudes, width)
    other_parts = spread(other_partial)
    sums = [
        total_of(parts).reshape(width, 2, parts.shape[2]) for parts in (own_parts, other_parts)
    ]
    (own_same, own_cross), (other_same, other_cross) = [(s[:, 0], s[:, 1]) for s in sums]
    first = core == 0

    def by_core(zero, one):
        return jnp.where(first, zero, one)

    even_a = jnp.stack([by_core(own_same, other_same), by_core(other_cross, own_cross)], axis=1)
    odd_a = jnp.stack([by_core(own_cross, other_cross), by_core(other_same, own_same)], axis=1)
    summed = jnp.stack([even_a, odd_a]).reshape(2 * full_width, amplitudes.shape[2])
    row_total = summed.shape[0]
    global_rows = lax.axis_index(("col", "dev")) * row_total + jnp.arange(
        row_total, dtype=jnp.int32
    )
    window_energy = select_energy(window_ids, vir_energy)
    energy_first = select_energy(global_rows // full_width, window_energy)
    energy_second = select_energy(global_rows % full_width, window_energy)
    energy_i = select_energy(pair_list[0], occ_energy)
    energy_j = select_energy(pair_list[1], occ_energy)
    denominator = (energy_i + energy_j)[None, :] - (energy_first + energy_second)[:, None]
    return summed / denominator


def on_device(raw_ints, *rest):
    cols, devs, cores = lax.axis_size("col"), lax.axis_size("dev"), lax.axis_size("ao")
    _, full_width, c_block = raw_ints.shape
    paired = cols == devs and cores == 2 and full_width == 2 * cols * devs
    if paired and cols & (cols - 1) == 0 and c_block % 128 == 0:
        return plan_on_device(raw_ints, *rest)
    return general_plan(raw_ints, *rest)


def solution(mesh):
    in_specs = (
        P("dev", None, "col"),
        P("dev", None),
        P("col", "dev", "ao"),
        P(None, "ao"),
        P(),
        P(),
        P(),
    )
    out_specs = P(("col", "dev"), "ao")
    return jax.shard_map(
        on_device, mesh=mesh, in_specs=in_specs, out_specs=out_specs, check_vma=False
    )
```

```python
import functools

import jax
import jax.numpy as jnp
from jax import lax
from jax.experimental import pallas as pl
from jax.experimental.pallas import tpu as pltpu
from jax.sharding import PartitionSpec as P


def select_energy(positions, table):
    labels = jnp.arange(table.shape[0], dtype=jnp.int32)
    return jnp.sum(jnp.where(positions[:, None] == labels[None, :], table[None, :], 0.0), axis=1)


def general_plan(raw_ints, metric, amplitudes, pair_list, occ_energy, vir_energy, window_ids):
    full_width = raw_ints.shape[1]
    portion = full_width // lax.axis_size("ao")
    own_rows = lax.dynamic_slice_in_dim(raw_ints, lax.axis_index("ao") * portion, portion, 1)
    local_aux = metric.shape[0]
    rows_used = own_rows.shape[1]
    c_block = own_rows.shape[2]
    raw_block = lax.all_gather(own_rows, "dev", axis=0, tiled=True)
    row_count = raw_block.shape[0]
    transformed = jnp.dot(
        metric,
        raw_block.reshape(row_count, rows_used * c_block),
        preferred_element_type=jnp.float32,
    )
    transformed = transformed.astype(jnp.bfloat16).reshape(local_aux, rows_used, c_block)
    spread = lax.all_gather(transformed, "col", axis=2, tiled=True)
    right_factor = lax.all_to_all(spread, "dev", split_axis=2, concat_axis=0, tiled=True)
    d_block = right_factor.shape[2]
    contract = (((0,), (0,)), ((), ()))
    left_factor = lax.all_gather(transformed, "dev", axis=0, tiled=True)
    right_factor = lax.all_gather(right_factor, "ao", axis=1, tiled=True)
    all_aux = left_factor.shape[0]
    own_ladder = lax.dot_general(
        left_factor.reshape(all_aux, rows_used * c_block),
        right_factor.reshape(all_aux, full_width * d_block),
        contract,
        preferred_element_type=jnp.float32,
    )
    ladder_flat = lax.all_gather(own_ladder.astype(jnp.bfloat16), "ao", axis=0, tiled=True)
    ladder = ladder_flat.reshape(full_width, c_block, full_width, d_block)
    ladder = jnp.transpose(ladder, (0, 2, 1, 3)).reshape(full_width * full_width, c_block * d_block)
    partial_value = jnp.dot(
        ladder,
        amplitudes.reshape(c_block * d_block, amplitudes.shape[2]),
        preferred_element_type=jnp.float32,
    )
    summed = lax.psum_scatter(partial_value, ("col", "dev"), scatter_dimension=0, tiled=True)
    row_total = summed.shape[0]
    global_rows = lax.axis_index(("col", "dev")) * row_total + jnp.arange(
        row_total, dtype=jnp.int32
    )
    window_energy = select_energy(window_ids, vir_energy)
    energy_first = select_energy(global_rows // full_width, window_energy)
    energy_second = select_energy(global_rows % full_width, window_energy)
    energy_i = select_energy(pair_list[0], occ_energy)
    energy_j = select_energy(pair_list[1], occ_energy)
    denominator = (energy_i + energy_j)[None, :] - (energy_first + energy_second)[:, None]
    return summed / denominator


VMEM = 62 * 1024 * 1024


def on_ring(piece, axis):
    count = lax.axis_size(axis)
    pairs = [(place, (place + 1) % count) for place in range(count)]
    return lax.ppermute(piece, axis, pairs)


def flip(piece, axis, bit):
    pairs = [(place, place ^ 1 << bit) for place in range(lax.axis_size(axis))]
    return lax.ppermute(piece, axis, pairs)


def bits_of(count):
    return count.bit_length() - 1


def metric_kernel(devs, place_ref, *refs):
    whole_ref, turned_ref = refs[-2:]
    pieces = refs[:-2]
    count = len(pieces) // 2
    rows, aux = pieces[0].shape
    core, dev = place_ref[0], place_ref[1]
    block = aux // devs
    for half in range(2):
        for at in range(count):
            row = pl.multiple_of(((core ^ half) * count + at) * rows, rows)
            for step in range(devs):
                column = pl.multiple_of(lax.rem(dev - step + devs, devs) * block, block)
                whole_ref[pl.ds(row, rows), step * block : (step + 1) * block] = pieces[
                    half * count + at
                ][:, pl.ds(column, block)]
    turned_ref[...] = whole_ref[...].T


def whole_metric(metric):
    cols, devs, cores = lax.axis_size("col"), lax.axis_size("dev"), lax.axis_size("ao")
    share = metric.shape[0] // (cols * cores)
    at = (lax.axis_index("col") * cores + lax.axis_index("ao")) * share
    shares = [lax.dynamic_slice_in_dim(metric, at, share, 0)]
    for step in range(1, devs):
        pairs = [(dev, (dev + step) % devs) for dev in range(devs)]
        shares.append(lax.ppermute(shares[0], "dev", pairs))
    rows = [jnp.concatenate(shares, axis=0)]
    for turn in range(1, cols):
        rows.append(lax.ppermute(rows[0], "col", [(col, col ^ turn) for col in range(cols)]))
    rows += [flip(rows[turn], "ao", 0) for turn in range(cols)]
    place = jnp.stack([lax.axis_index("ao"), lax.axis_index("dev")]).astype(jnp.int32)
    shape = jax.ShapeDtypeStruct((metric.shape[0] * devs, metric.shape[1]), metric.dtype)
    return pl.pallas_call(
        functools.partial(metric_kernel, devs),
        in_specs=[pl.BlockSpec(memory_space=pltpu.SMEM)]
        + [pl.BlockSpec(memory_space=pltpu.VMEM)] * len(rows),
        out_specs=[pl.BlockSpec(memory_space=pltpu.VMEM)] * 2,
        out_shape=[shape, jax.ShapeDtypeStruct(shape.shape[::-1], metric.dtype)],
        compiler_params=pltpu.CompilerParams(vmem_limit_bytes=VMEM),
    )(place, *rows)


def left_kernel(metric_ref, *refs):
    rows = jnp.concatenate([ref[...] for ref in refs[:-1]], axis=2)
    count, width, depth = rows.shape
    product = jnp.dot(
        rows.reshape(count * width, depth), metric_ref[...], preferred_element_type=jnp.float32
    )
    refs[-1][...] = product.astype(jnp.bfloat16).reshape(count, width, product.shape[1])


def fit_left(metric_turned, pieces):
    c_block, width, depth = pieces[0].shape
    step = 32
    aux = metric_turned.shape[1]
    piece_spec = pl.BlockSpec((step, width, depth), lambda i: (i, 0, 0))
    return pl.pallas_call(
        left_kernel,
        grid=(c_block // step,),
        in_specs=[pl.BlockSpec(metric_turned.shape, lambda i: (0, 0))] + [piece_spec] * len(pieces),
        out_specs=pl.BlockSpec((step, width, aux), lambda i: (i, 0, 0)),
        out_shape=jax.ShapeDtypeStruct((c_block, width, aux), jnp.bfloat16),
        compiler_params=pltpu.CompilerParams(vmem_limit_bytes=VMEM),
        cost_estimate=pl.CostEstimate(
            flops=2 * metric_turned.size * c_block * width,
            bytes_accessed=2 * (metric_turned.size + 2 * c_block * width * aux),
            transcendentals=0,
        ),
    )(metric_turned, *pieces)


def fit_kernel(arrived_ref, metric_ref, *refs):
    out_ref, held, sems = refs[-3:]
    pieces = refs[:-3]
    count = len(pieces) // 2
    width = held.shape[2]
    step = pl.program_id(0)

    def fetch(at, slot):
        for piece in range(count):
            for came in range(2):

                @pl.when(arrived_ref[piece % 2] == came)
                def _(piece=piece, came=came):
                    pltpu.make_async_copy(
                        pieces[2 * piece + came].at[pl.ds(at * width, width)],
                        held.at[slot, piece],
                        sems.at[slot, piece],
                    ).start()

    @pl.when(step == 0)
    def _():
        fetch(0, 0)

    slot = lax.rem(step, 2)

    @pl.when(step + 1 < pl.num_programs(0))
    def _():
        fetch(step + 1, 1 - slot)

    for piece in range(count):
        pltpu.make_async_copy(
            pieces[2 * piece].at[pl.ds(step * width, width)],
            held.at[slot, piece],
            sems.at[slot, piece],
        ).wait()
    columns = [
        jnp.concatenate([held[slot, piece, b] for piece in range(count)], axis=0)
        for b in range(width)
    ]
    out_ref[...] = jnp.dot(
        metric_ref[...], jnp.concatenate(columns, axis=1), preferred_element_type=jnp.float32
    ).astype(out_ref.dtype)


def fit_right(arrived, metric_all, flat):
    width, depth, d_block = flat[0].shape
    step = 4
    aux = metric_all.shape[0]
    count = len(flat) // 2
    part = count * depth
    return pl.pallas_call(
        fit_kernel,
        grid=(width // step,),
        in_specs=[
            pl.BlockSpec(memory_space=pltpu.SMEM),
            pl.BlockSpec((aux, part), lambda i: (0, 0)),
        ]
        + [pl.BlockSpec(memory_space=pl.ANY)] * len(flat),
        out_specs=pl.BlockSpec((aux, step * d_block), lambda i: (0, i)),
        out_shape=jax.ShapeDtypeStruct((aux, width * d_block), jnp.float32),
        scratch_shapes=[
            pltpu.VMEM((2, count, step, depth, d_block), jnp.bfloat16),
            pltpu.SemaphoreType.DMA((2, count)),
        ],
        compiler_params=pltpu.CompilerParams(vmem_limit_bytes=24 * 1024 * 1024),
        cost_estimate=pl.CostEstimate(
            flops=2 * aux * part * width * d_block,
            bytes_accessed=2 * (aux * part + count * flat[0].size + 2 * aux * width * d_block),
            transcendentals=0,
        ),
    )(arrived, metric_all, *flat)


def ladder_kernel(
    arrived_ref, metric_ref, own_ref, other_ref, early_ref, *refs
):
    ladder_ref, right_ref, sums_ref, held, sum_sems, sems = refs[-6:]
    pieces = refs[:-6]
    count = len(pieces) // 2
    c_count, width, depth = own_ref.shape
    d_block = ladder_ref.shape[1] // c_count
    right_rows = right_ref.shape[1] // d_block
    parts, _, columns = sums_ref.shape

    @pl.when(pl.program_id(0) == 0)
    def _():
        for piece in range(count):
            for came in range(2):

                @pl.when(arrived_ref[piece % 2] == came)
                def _(piece=piece, came=came):
                    pltpu.make_async_copy(
                        pieces[2 * piece + came], held.at[piece], sems.at[piece]
                    ).start()

        fetched = [
            pltpu.make_async_copy(
                early_ref.at[:, pl.ds(part * columns, columns)], sums_ref.at[part], sum_sems.at[part]
            )
            for part in range(parts)
        ]
        for copy in fetched:
            copy.start()
        for piece in range(count):
            pltpu.make_async_copy(pieces[2 * piece], held.at[piece], sems.at[piece]).wait()
        many = columns // d_block
        for part in range(parts):
            fetched[part].wait()
            late = [
                jnp.concatenate([held[piece, part * many + b] for piece in range(count)], axis=0)
                for b in range(many)
            ]
            product = jnp.dot(
                metric_ref[...], jnp.concatenate(late, axis=1), preferred_element_type=jnp.float32
            )
            right_ref[:, part * columns : (part + 1) * columns] = (
                product + sums_ref[part]
            ).astype(right_ref.dtype)

    for half, ref in enumerate((own_ref, other_ref)):
        product = jnp.dot(
            ref[...].reshape(c_count * width, depth),
            right_ref[...],
            preferred_element_type=jnp.float32,
        ).astype(jnp.bfloat16)
        for c in range(c_count):
            for b in range(right_rows):
                row = (b * 2 + half) * width
                ladder_ref[row : row + width, c * d_block : (c + 1) * d_block] = product[
                    c * width : (c + 1) * width, b * d_block : (b + 1) * d_block
                ]


def ladder_of(arrived, metric_all, own_left, other_left, early, flat):
    c_block, width, depth = own_left.shape
    right_rows, rows_late, d_block = flat[0].shape
    step, parts = 16, 4
    count = len(flat) // 2
    part = count * rows_late
    aux, columns = early.shape
    left_spec = pl.BlockSpec((step, width, depth), lambda i: (i, 0, 0))
    rows = right_rows * 2 * width
    return pl.pallas_call(
        ladder_kernel,
        grid=(c_block // step,),
        in_specs=[
            pl.BlockSpec(memory_space=pltpu.SMEM),
            pl.BlockSpec((aux, part), lambda i: (0, metric_all.shape[1] // part - 1)),
            left_spec,
            left_spec,
        ]
        + [pl.BlockSpec(memory_space=pl.ANY)] * (1 + len(flat)),
        out_specs=pl.BlockSpec((rows, step * d_block), lambda i: (0, i)),
        out_shape=jax.ShapeDtypeStruct((rows, c_block * d_block), jnp.bfloat16),
        scratch_shapes=[
            pltpu.VMEM((aux, columns), jnp.bfloat16),
            pltpu.VMEM((parts, aux, columns // parts), jnp.float32),
            pltpu.VMEM((count, right_rows, rows_late, d_block), jnp.bfloat16),
            pltpu.SemaphoreType.DMA((parts,)),
            pltpu.SemaphoreType.DMA((count,)),
        ],
        compiler_params=pltpu.CompilerParams(vmem_limit_bytes=30 * 1024 * 1024),
        cost_estimate=pl.CostEstimate(
            flops=4 * c_block * width * depth * columns + 2 * aux * part * columns,
            bytes_accessed=2 * (2 * own_left.size + 2 * early.size + rows * c_block * d_block),
            transcendentals=0,
        ),
    )(arrived, metric_all, own_left, other_left, early, *flat)


def contract_kernel(ladder_ref, amplitudes_ref, out_ref, total_ref):
    @pl.when(pl.program_id(0) == 0)
    def _():
        total_ref[...] = jnp.zeros_like(total_ref)

    product = jnp.dot(ladder_ref[...], amplitudes_ref[...], preferred_element_type=jnp.float32)
    tiles, _, lanes = total_ref.shape
    for tile in range(tiles):
        total_ref[tile] += product[:, tile * lanes : (tile + 1) * lanes]

    @pl.when(pl.program_id(0) == pl.num_programs(0) - 1)
    def _():
        owners, rows, _ = out_ref.shape
        for owner in range(owners):
            for tile in range(tiles):
                out_ref[owner, :, tile * lanes : (tile + 1) * lanes] = total_ref[
                    tile, pl.ds(owner, rows, stride=owners), :
                ].astype(out_ref.dtype)


def contract(ladder, amplitudes, owners):
    rows, depth = ladder.shape
    columns = amplitudes.shape[1]
    step = 4096
    return pl.pallas_call(
        contract_kernel,
        grid=(depth // step,),
        in_specs=[
            pl.BlockSpec((rows, step), lambda i: (0, i)),
            pl.BlockSpec((step, columns), lambda i: (i, 0)),
        ],
        out_specs=pl.BlockSpec((owners, rows // owners, columns), lambda i: (0, 0, 0)),
        out_shape=jax.ShapeDtypeStruct((owners, rows // owners, columns), jnp.bfloat16),
        scratch_shapes=[pltpu.VMEM((columns // 128, rows, 128), jnp.float32)],
        compiler_params=pltpu.CompilerParams(vmem_limit_bytes=40 * 1024 * 1024),
        cost_estimate=pl.CostEstimate(
            flops=2 * rows * depth * columns,
            bytes_accessed=2 * (rows * depth + depth * columns + rows * columns),
            transcendentals=0,
        ),
    )(ladder, amplitudes)


def spread(partial):
    return lax.all_to_all(partial, ("col", "dev"), split_axis=0, concat_axis=0, tiled=True)


def spread_twice(partial):
    cols, devs = lax.axis_size("col"), lax.axis_size("dev")
    plane = lax.all_to_all(partial, "col", split_axis=0, concat_axis=0, tiled=True)
    plane = total_of(plane.reshape(cols, devs, *partial.shape[1:])).astype(partial.dtype)
    return lax.all_to_all(plane, "dev", split_axis=0, concat_axis=0, tiled=True)


def total_of(parts):
    return jnp.sum(parts.astype(jnp.float32), axis=0)


def plan_on_device(raw_ints, metric, amplitudes, pair_list, occ_energy, vir_energy, window_ids):
    aux, full_width, c_block = raw_ints.shape
    cols, devs = lax.axis_size("col"), lax.axis_size("dev")
    core = lax.axis_index("ao")
    width = full_width // 2
    own = lax.dynamic_index_in_dim(raw_ints.reshape(aux, width, 2, c_block), core, 2, keepdims=False)
    own = jnp.transpose(own, (1, 0, 2))
    half = aux // 2
    here = list(lax.optimization_barrier((own[:, :half], own[:, half:])))
    metric_all, metric_turned = whole_metric(metric)
    away = lax.axis_index("col") ^ lax.axis_index("dev")
    bits = bits_of(cols)
    bit_set = [(away >> bit) & 1 for bit in range(bits)]
    came = [flag == 1 for flag in bit_set]
    *came, away = lax.optimization_barrier((*came, away))
    arrived = jnp.stack([bit_set[(h + bits - 1) % bits] for h in range(2)]).astype(jnp.int32)
    pieces, left_pieces = [], []
    for s in range(devs):
        for h in range(2):
            left_pieces.append(jnp.transpose(here[h], (2, 0, 1)))
        if s < devs - 1:
            ahead = [on_ring(here[h], "dev") for h in range(2)]
        else:
            own_left = fit_left(metric_turned, left_pieces)
        held = here
        for hop in range(bits):
            if hop:
                held = [
                    jnp.where(came[(h + hop - 1) % bits], last[h], held[h]) for h in range(2)
                ]
                held = list(lax.optimization_barrier(tuple(held)))
            last = [flip(held[h], "col", (h + hop) % bits) for h in range(2)]
        pieces += [held[0], last[0], held[1], last[1]]
        here = ahead
    other_left = flip(own_left, "ao", 0)
    early = fit_right(arrived, metric_all, pieces[:-4])
    own_ladder = ladder_of(arrived, metric_all, own_left, other_left, early, pieces[-4:])
    other_ladder = flip(own_ladder, "ao", 0)
    flat_amplitudes = amplitudes.reshape(c_block * amplitudes.shape[1], amplitudes.shape[2])
    own_partial = contract(own_ladder, flat_amplitudes, width)
    own_parts = spread(own_partial)
    other_partial = contract(other_ladder, flat_amplitudes, width)
    other_parts = spread_twice(other_partial)
    sums = [
        total_of(parts).reshape(width, 2, parts.shape[2]) for parts in (own_parts, other_parts)
    ]
    (own_same, own_cross), (other_same, other_cross) = [(s[:, 0], s[:, 1]) for s in sums]
    first = core == 0

    def by_core(zero, one):
        return jnp.where(first, zero, one)

    even_a = jnp.stack([by_core(own_same, other_same), by_core(other_cross, own_cross)], axis=1)
    odd_a = jnp.stack([by_core(own_cross, other_cross), by_core(other_same, own_same)], axis=1)
    summed = jnp.stack([even_a, odd_a]).reshape(2 * full_width, amplitudes.shape[2])
    row_total = summed.shape[0]
    global_rows = lax.axis_index(("col", "dev")) * row_total + jnp.arange(
        row_total, dtype=jnp.int32
    )
    window_energy = select_energy(window_ids, vir_energy)
    energy_first = select_energy(global_rows // full_width, window_energy)
    energy_second = select_energy(global_rows % full_width, window_energy)
    energy_i = select_energy(pair_list[0], occ_energy)
    energy_j = select_energy(pair_list[1], occ_energy)
    denominator = (energy_i + energy_j)[None, :] - (energy_first + energy_second)[:, None]
    return summed / denominator


def on_device(raw_ints, *rest):
    cols, devs, cores = lax.axis_size("col"), lax.axis_size("dev"), lax.axis_size("ao")
    _, full_width, c_block = raw_ints.shape
    paired = cols == devs and cores == 2 and full_width == 2 * cols * devs
    if paired and cols & (cols - 1) == 0 and c_block % 128 == 0:
        return plan_on_device(raw_ints, *rest)
    return general_plan(raw_ints, *rest)


def solution(mesh):
    in_specs = (
        P("dev", None, "col"),
        P("dev", None),
        P("col", "dev", "ao"),
        P(None, "ao"),
        P(),
        P(),
        P(),
    )
    out_specs = P(("col", "dev"), "ao")
    return jax.shard_map(
        on_device, mesh=mesh, in_specs=in_specs, out_specs=out_specs, check_vma=False
    )
```
